32 devices in a mesh: view: 4 (over x, core), depth: 8 (over z, y).
Axes of the slice: x: 2, y: 2, z: 4, core: 2. Of those that a mesh axis runs over, the one named last changes fastest.
Arguments:
- features: float32 [4, 8, 32, 3, 4096], P('view', 'depth'), may hold values from -6 to 6
- spacing: float32 [4, 8, 3, 4096], P('view', 'depth'), may hold values from 0.01 to 0.15
- counts: int32 [4, 8, 4096], P('view', 'depth'), may hold values from 0 to 3
- depth_rank: int32 [4, 8], P('view', 'depth'), may hold values from 0 to 7, as said below
- target: float32 [4, 64, 4096], P('view', None, 'depth'), may hold values from 0 to 1
- first_weight: float32 [32, 256], replicated, may hold values from -1 to 1
- first_bias: float32 [256], replicated, may hold values from -3 to 3
- second_weight: float32 [256, 256], replicated, may hold values from -0.375 to 0.375
- second_bias: float32 [256], replicated, may hold values from -3 to 3
- last_weight: float32 [256, 65], replicated, may hold values from -0.375 to 0.375
- last_bias: float32 [65], replicated, may hold values from -3 to 3
Outputs:
- pixels: float32 [4, 64, 4096], P('view', None, 'depth')
- first_update: float32 [32, 256], replicated
- first_shift: float32 [256], replicated
- second_update: float32 [256, 256], replicated
- second_shift: float32 [256], replicated
- last_update: float32 [256, 65], replicated
- last_shift: float32 [65], replicated
The draws below stay inside these ranges and needn't reach their ends.
Inputs may be any that keep to these rules, and one draw needn't show every extreme that they name: depth_rank[v, d] equals d XOR a number fixed for view group v, so each view group's ranks are a permutation in which every aligned block of 2^k regions takes consecutive positions. Sample slots s with s < counts[v, d, r] are live.
All inputs are finite; a program needn't handle non-finite values.
Results may differ from the reference program's by a relative error of at most 0.0003.
Values sent between devices are 32-bit elements; how exact they have to be, the bound alone decides.
A program may use at most 128 MiB of HBM per device.

```python
import math
import jax
import jax.numpy as jnp
from jax import lax

FEAT = 32
HIDDEN_SIZE = 256
CHANNELS = 64
SAMPLES = 3
RAYS = 4096
OUT = 65
VIEWS = 4
REGIONS = 8


def draw_depth_rank(key, part):
    region_ids = jnp.arange(REGIONS, dtype=jnp.int32)
    flips = jax.random.randint(jax.random.fold_in(key, 17), (VIEWS, 1), 0, REGIONS).astype(jnp.int32)
    return jnp.bitwise_xor(region_ids[None, :], flips).astype(jnp.int32)


def plant(entries, key, low, high):
    longest = entries.shape.index(max(entries.shape))
    spots = []
    for shift in (0, 1):
        where = [jax.random.randint(jax.random.fold_in(key, axis), (), 0, length) for axis, length in enumerate(entries.shape)]
        where[longest] = (where[longest] + shift) % entries.shape[longest]
        spots.append(tuple(where))
    return entries.at[spots[0]].set(low).at[spots[1]].set(high)


def block_scale(rng, extent, shards, low, high):
    gain = 1.0
    for dim, shards_of in shards:
        steps = jax.random.uniform(jax.random.fold_in(jax.random.fold_in(rng, 6), dim), (shards_of,), jnp.float32, low / len(shards), high / len(shards))
        gain = gain * jnp.repeat(jnp.exp(steps), extent[dim] // shards_of).reshape((-1,) + (1,) * (len(extent) - 1 - dim))
    return gain


def normal_values(own_key, shape, deviation, most, pieces=(), kind=jnp.bfloat16):
    entries = jax.random.normal(own_key, shape, jnp.float32) * deviation
    if len(pieces) > 0:
        entries = block_scale(own_key, shape, pieces, -0.22, 0.18) * entries
    return jnp.clip(entries, min=-most, max=most).astype(kind)


def setup_inputs(seed: int = 0) -> dict:
    key_of = jax.random.split(jax.random.key(seed), 12)
    features = normal_values(key_of[0], (VIEWS, REGIONS, FEAT, SAMPLES, RAYS), 1.0, 6.0, ((0, 4), (1, 8)), jnp.float32)
    spacing = jnp.clip(jnp.exp(math.log(0.15) - 2.7080503 * jax.random.uniform(key_of[1], (VIEWS, REGIONS, SAMPLES, RAYS), jnp.float32) ** block_scale(key_of[1], (VIEWS, REGIONS, SAMPLES, RAYS), ((0, 4), (1, 8)), -0.2, 0.2)), 0.01, 0.15)
    counts = plant(jax.random.randint(key_of[2], (VIEWS, REGIONS, RAYS), 0, SAMPLES + 1), jax.random.fold_in(key_of[2], 1), 0, SAMPLES).astype(jnp.int32)
    depth_rank = draw_depth_rank(jax.random.fold_in(key_of[11], 71), 0)
    target = jnp.clip(1.0 * jax.random.uniform(key_of[4], (VIEWS, CHANNELS, RAYS), jnp.float32) ** block_scale(key_of[4], (VIEWS, CHANNELS, RAYS), ((0, 4), (2, 8)), -0.2, 0.2), 0.0, 1.0)
    first_weight = normal_values(key_of[5], (FEAT, HIDDEN_SIZE), FEAT ** -0.5, 1.0, (), jnp.float32)
    first_bias = normal_values(key_of[6], (HIDDEN_SIZE,), 0.5, 3.0, (), jnp.float32)
    second_weight = normal_values(key_of[7], (HIDDEN_SIZE, HIDDEN_SIZE), HIDDEN_SIZE ** -0.5, 0.375, (), jnp.float32)
    second_bias = normal_values(key_of[8], (HIDDEN_SIZE,), 0.5, 3.0, (), jnp.float32)
    last_weight = normal_values(key_of[9], (HIDDEN_SIZE, OUT), HIDDEN_SIZE ** -0.5, 0.375, (), jnp.float32)
    last_bias = normal_values(key_of[10], (OUT,), 0.5, 3.0, (), jnp.float32)
    return {"features": features, "spacing": spacing, "counts": counts, "depth_rank": depth_rank, "target": target, "first_weight": first_weight, "first_bias": first_bias, "second_weight": second_weight, "second_bias": second_bias, "last_weight": last_weight, "last_bias": last_bias}


precise = lax.Precision.HIGHEST
epsilon = 1e-05

def project(weight, inputs):
    return lax.dot_general(weight, inputs, (((0,), (0,)), ((), ())), precision=precise, preferred_element_type=jnp.float32)

def render(params, sample_feats, sample_spacing, live_mask):
    first_weight, first_bias, second_weight, second_bias, last_weight, last_bias = params
    columns = sample_feats.reshape(sample_feats.shape[0], -1)
    first_act = jax.nn.relu(project(first_weight, columns) + first_bias[:, None])
    second_act = jax.nn.relu(project(second_weight, first_act) + second_bias[:, None])
    raw_output = project(last_weight, second_act) + last_bias[:, None]
    raw_output = raw_output.reshape(raw_output.shape[0], sample_spacing.shape[0], sample_spacing.shape[1])
    channels = raw_output.shape[0] - 1
    sample_color = jax.nn.sigmoid(raw_output[:channels])
    density = jax.nn.softplus(raw_output[channels])
    optical = density * sample_spacing * live_mask
    before = jnp.cumsum(optical, axis=0) - optical
    weight = jnp.exp(-before) * (1.0 - jnp.exp(-optical))
    region_color = lax.optimization_barrier(jnp.sum(weight[None] * sample_color, axis=1))
    region_depth = lax.optimization_barrier(jnp.sum(optical, axis=0))
    return (region_color, region_depth)

def normalize(gradient):
    return gradient / jnp.sqrt(jnp.mean(gradient * gradient) + epsilon)

def reference(features, spacing, counts, depth_rank, target, first_weight, first_bias, second_weight, second_bias, last_weight, last_bias):
    params = (first_weight, first_bias, second_weight, second_bias, last_weight, last_bias)
    sample_ids = jnp.arange(SAMPLES, dtype=jnp.int32)
    live_mask = (sample_ids[None, None, :, None] < counts[:, :, None, :]).astype(jnp.float32)
    flat_feats = features.reshape(VIEWS * REGIONS, FEAT, SAMPLES, RAYS)
    flat_spacing = spacing.reshape(VIEWS * REGIONS, SAMPLES, RAYS)
    flat_live = live_mask.reshape(VIEWS * REGIONS, SAMPLES, RAYS)

    def forward(scan_items):
        return render(params, scan_items[0], scan_items[1], scan_items[2])
    colors, depths = lax.map(forward, (flat_feats, flat_spacing, flat_live))
    colors = colors.reshape(VIEWS, REGIONS, CHANNELS, RAYS)
    depths = depths.reshape(VIEWS, REGIONS, RAYS)
    earlier = (depth_rank[:, None, :] < depth_rank[:, :, None]).astype(jnp.float32)
    later_mask = (depth_rank[:, None, :] > depth_rank[:, :, None]).astype(jnp.float32)
    passed = jnp.exp(-jnp.einsum('vde,ver->vdr', earlier, depths, precision=precise))
    weighted = passed[:, :, None, :] * colors
    pixels = lax.optimization_barrier(jnp.sum(weighted, axis=1))
    misfit = pixels - target
    color_grad = passed[:, :, None, :] * misfit[:, None]
    behind = jnp.einsum('vde,vecr->vdcr', later_mask, weighted, precision=precise)
    depth_grad = -lax.optimization_barrier(jnp.sum(misfit[:, None] * behind, axis=2))

    def accumulate(running, scan_items):
        sample_feats, sample_spacing, live_part, color_part, depth_part = scan_items
        unused, pullback = jax.vjp(lambda weights: render(weights, sample_feats, sample_spacing, live_part), params)
        gradients = pullback((color_part, depth_part))[0]
        return (jax.tree.map(jnp.add, running, gradients), None)
    zero_grads = jax.tree.map(jnp.zeros_like, params)
    totals, unused_out = lax.scan(accumulate, zero_grads, (flat_feats, flat_spacing, flat_live, color_grad.reshape(VIEWS * REGIONS, CHANNELS, RAYS), depth_grad.reshape(VIEWS * REGIONS, RAYS)))
    return (pixels, normalize(totals[0]), normalize(totals[1]), normalize(totals[2]), normalize(totals[3]), normalize(totals[4]), normalize(totals[5]))
```

```python
import functools

import jax
import jax.numpy as jnp
from jax import lax
from jax.experimental import pallas as pl
from jax.experimental.pallas import tpu as pltpu
from jax.sharding import PartitionSpec as P

epsilon = 1e-05
PAD = 80
MESH = pl.DeviceIdType.MESH
f32 = jnp.float32
bf16 = jnp.bfloat16


def split(value):
    high = value.astype(bf16)
    low = (value - high.astype(f32)).astype(bf16)
    return high, low


def mm(left, right):
    return lax.dot_general(left, right, (((1,), (0,)), ((), ())), preferred_element_type=f32)


def mm_nt(left, right):
    return lax.dot_general(left, right, (((1,), (1,)), ((), ())), preferred_element_type=f32)


def opticals(raw, channels, spacing, counts, samples, rays):
    out = []
    for s in range(samples):
        logit = raw[channels : channels + 1, s * rays : (s + 1) * rays]
        density = jnp.maximum(logit, 0.0) + jnp.log1p(jnp.exp(-jnp.abs(logit)))
        length = jnp.where(s < counts, spacing[s : s + 1, :], 0.0)
        out.append((logit, density * length, length))
    return out


def forward_kernel(
    feats_ref, spacing_ref, counts_ref, w1_ref, b1_ref, w2_ref, b2_ref, w3_ref, b3_ref,
    packed_ref, hidden_ref, raw_ref,
    pack, w1s, w2s, w3s, cols,
):
    feat, samples, rays = feats_ref.shape
    hidden = w2_ref.shape[0]
    outs = w3_ref.shape[1]
    channels = outs - 1

    @pl.when(pl.program_id(0) == 0)
    def _():
        pack[...] = jnp.zeros_like(pack)
        high, low = split(w1_ref[...])
        pack[0:feat, :] = high.astype(f32)
        pack[feat : 2 * feat, :] = high.astype(f32)
        pack[2 * feat : 3 * feat, :] = low.astype(f32)
        bias = b1_ref[...]
        bias_a = bias.astype(bf16).astype(f32)
        bias_b = (bias - bias_a).astype(bf16).astype(f32)
        pack[3 * feat : 3 * feat + 1, :] = bias_a
        pack[3 * feat + 1 : 3 * feat + 2, :] = bias_b
        pack[3 * feat + 2 : 3 * feat + 3, :] = bias - bias_a - bias_b
        pack[3 * feat + 3 : 3 * feat + 4, :] = b2_ref[...]
        pack[3 * feat + 4 : 3 * feat + 5, 0:outs] = b3_ref[...]
        turned = pack[...].T
        w1s[...] = turned.astype(bf16)
        cols[...] = turned
        high, low = split(w2_ref[...].T)
        w2s[:, 0:hidden] = high
        w2s[:, hidden : 2 * hidden] = high
        w2s[:, 2 * hidden : 3 * hidden] = low
        pack[...] = jnp.zeros_like(pack)
        tall = jnp.concatenate(
            [w3_ref[...], jnp.zeros((hidden, 128 - outs), f32)], axis=1
        ).T
        high, low = split(tall[0:PAD, :])
        w3s[0:PAD, :] = high
        w3s[PAD : 2 * PAD, :] = low

    x = jnp.concatenate([feats_ref[:, s, :] for s in range(samples)], axis=1)
    xh, xl = split(x)
    rows = lax.broadcasted_iota(jnp.int32, x.shape, 0)
    ones = jnp.where(rows < 3, 1.0, 0.0).astype(bf16)
    z1 = mm(w1s[...], jnp.concatenate([xh, xl, xh, ones], axis=0))
    h1h, h1l = split(jnp.maximum(z1, 0.0))
    hidden_ref[0, 0] = h1h
    hidden_ref[0, 1] = h1l
    z2 = mm(w2s[...], jnp.concatenate([h1h, h1l, h1h], axis=0))
    z2 = z2 + cols[:, 3 * feat + 3 : 3 * feat + 4]
    h2h, h2l = split(jnp.maximum(z2, 0.0))
    hidden_ref[0, 2] = h2h
    hidden_ref[0, 3] = h2l
    both = mm(w3s[...], h2h)
    raw = both[0:PAD] + both[PAD:] + mm(w3s[0:PAD, :], h2l)
    raw = raw + cols[0:PAD, 3 * feat + 4 : 3 * feat + 5]
    raw_ref[0] = raw
    before = None
    color = None
    for s, (_, optical, _) in enumerate(
        opticals(raw, channels, spacing_ref[...], counts_ref[...], samples, rays)
    ):
        weight = 1.0 - jnp.exp(-optical)
        if s:
            weight = jnp.exp(-before) * weight
        shade = weight * jax.nn.sigmoid(raw[0:channels, s * rays : (s + 1) * rays])
        color = shade if s == 0 else color + shade
        before = optical if s == 0 else before + optical
    packed_ref[0, 0:channels] = color
    packed_ref[0, channels : channels + 8] = jnp.broadcast_to(before, (8, rays))


def forward(features, spacing, counts, weights, regions):
    feat, samples, total = features.shape
    rays = total // regions
    hidden = weights[2].shape[0]
    outs = weights[4].shape[1]
    wide = samples * rays
    whole = lambda a: pl.BlockSpec(a.shape, lambda t: (0,) * a.ndim)
    return pl.pallas_call(
        forward_kernel,
        grid=(regions,),
        in_specs=[
            pl.BlockSpec((feat, samples, rays), lambda t: (0, 0, t)),
            pl.BlockSpec((samples, rays), lambda t: (0, t)),
            pl.BlockSpec((1, rays), lambda t: (0, t)),
        ]
        + [whole(a) for a in weights],
        out_specs=[
            pl.BlockSpec((1, outs + 7, rays), lambda t: (t, 0, 0)),
            pl.BlockSpec((1, 4, hidden, wide), lambda t: (t, 0, 0, 0)),
            pl.BlockSpec((1, PAD, wide), lambda t: (t, 0, 0)),
        ],
        out_shape=[
            jax.ShapeDtypeStruct((regions, outs + 7, rays), f32),
            jax.ShapeDtypeStruct((regions, 4, hidden, wide), bf16),
            jax.ShapeDtypeStruct((regions, PAD, wide), f32),
        ],
        scratch_shapes=[
            pltpu.VMEM((128, hidden), f32),
            pltpu.VMEM((hidden, 128), bf16),
            pltpu.VMEM((hidden, 3 * hidden), bf16),
            pltpu.VMEM((2 * PAD, hidden), bf16),
            pltpu.VMEM((hidden, 128), f32),
        ],
        name="render_forward",
    )(features, spacing, counts, *weights)


def backward_kernel(
    feats_ref, spacing_ref, counts_ref, w2_ref, w3_ref, hidden_ref, raw_ref, back_ref,
    out_ref,
    w2s, w3s, acc1, acc2, acc3, bias,
):
    feat, samples, rays = feats_ref.shape
    hidden = w2_ref.shape[0]
    outs = w3_ref.shape[1]
    channels = outs - 1
    step = pl.program_id(0)

    @pl.when(step == 0)
    def _():
        high, low = split(w2_ref[...])
        w2s[:, 0:hidden] = high
        w2s[:, hidden : 2 * hidden] = high
        w2s[:, 2 * hidden : 3 * hidden] = low
        tall = jnp.concatenate(
            [w3_ref[...], jnp.zeros((hidden, 128 - outs), f32)], axis=1
        ).T[0:PAD, :]
        high = tall.astype(bf16).astype(f32)
        stack = jnp.concatenate(
            [high, high, tall - high, jnp.zeros((256 - 3 * PAD, hidden), f32)], axis=0
        )
        w3s[...] = stack.T.astype(bf16)
        acc1[...] = jnp.zeros_like(acc1)
        acc2[...] = jnp.zeros_like(acc2)
        acc3[...] = jnp.zeros_like(acc3)
        bias[...] = jnp.zeros_like(bias)

    raw = raw_ref[0]
    misfit = back_ref[0, 0:channels]
    passed = back_ref[0, channels : channels + 1]
    depth_grad = -back_ref[0, channels + 1 : channels + 2]
    parts = opticals(raw, channels, spacing_ref[...], counts_ref[...], samples, rays)
    befores, before = [], None
    for s in range(samples):
        befores.append(before)
        before = parts[s][1] if s == 0 else before + parts[s][1]
    tail = depth_grad
    pieces = [None] * samples
    for s in reversed(range(samples)):
        logit, optical, length = parts[s]
        gone = jnp.exp(-optical)
        ahead = 1.0 if s == 0 else jnp.exp(-befores[s])
        weight = ahead * (1.0 - gone)
        color = jax.nn.sigmoid(raw[0:channels, s * rays : (s + 1) * rays])
        weight_grad = passed * jnp.sum(misfit * color, axis=0, keepdims=True)
        optical_grad = weight_grad * (ahead * gone) + tail
        tail = tail - weight_grad * weight
        color_grad = (weight * passed) * misfit * (color * (1.0 - color))
        logit_grad = optical_grad * length * jax.nn.sigmoid(logit)
        row = lax.broadcasted_iota(jnp.int32, (PAD - channels, rays), 0)
        rest = jnp.where(row == 0, jnp.broadcast_to(logit_grad, row.shape), 0.0)
        pieces[s] = jnp.concatenate([color_grad, rest], axis=0)
    draw = jnp.concatenate(pieces, axis=1)
    bias[2 * hidden : 2 * hidden + PAD, :] += lanes(draw)
    dh, dl = split(draw)
    h2h = hidden_ref[0, 2]
    h2l = hidden_ref[0, 3]
    both = mm_nt(jnp.concatenate([dh, dl], axis=0), h2h)
    acc3[...] += both[0:PAD] + both[PAD:] + mm_nt(dh, h2l)
    zero = jnp.zeros((256 - 3 * PAD, draw.shape[1]), bf16)
    dh2 = mm(w3s[...], jnp.concatenate([dh, dl, dh, zero], axis=0))
    dz2 = jnp.where(h2h > 0, dh2, 0.0)
    bias[hidden : 2 * hidden, :] += lanes(dz2)
    zh, zl = split(dz2)
    h1h = hidden_ref[0, 0]
    h1l = hidden_ref[0, 1]
    acc2[...] += mm_nt(h1h, zh) + mm_nt(h1l, zh) + mm_nt(h1h, zl)
    dh1 = mm(w2s[...], jnp.concatenate([zh, zl, zh], axis=0))
    dz1 = jnp.where(h1h > 0, dh1, 0.0)
    bias[0:hidden, :] += lanes(dz1)
    x = jnp.concatenate([feats_ref[:, s, :] for s in range(samples)], axis=1)
    xh, xl = split(x)
    zh, zl = split(dz1)
    both = mm_nt(jnp.concatenate([xh, xl], axis=0), zh)
    acc1[...] += both[0:feat] + both[feat:] + mm_nt(xh, zl)

    @pl.when(step == pl.num_programs(0) - 1)
    def _():
        out_ref[...] = jnp.zeros_like(out_ref)
        at = 0
        for acc in (acc2, acc1, acc3):
            rows = acc.shape[0]
            for lane in range(0, hidden, 128):
                blocks = rows // 8
                out_ref[at : at + blocks] = acc[:, lane : lane + 128].reshape(blocks, 8, 128)
                at += blocks
        sums = jnp.sum(bias[...].T, axis=0, keepdims=True)
        for lane in range(5):
            out_ref[at, lane : lane + 1, :] = sums[:, lane * 128 : (lane + 1) * 128]


def lanes(value):
    total = value[:, 0:128]
    for lane in range(128, value.shape[1], 128):
        total = total + value[:, lane : lane + 128]
    return total


def block_count(feat, hidden, devices):
    blocks = (hidden + feat + PAD) // 8 * (hidden // 128) + 1
    return -(-blocks // devices) * devices


def backward(features, spacing, counts, w2, w3, hiddens, raws, backs, blocks):
    feat, samples, total = features.shape
    regions, rows, rays = backs.shape
    hidden = w2.shape[0]
    wide = samples * rays
    whole = lambda a: pl.BlockSpec(a.shape, lambda t: (0,) * a.ndim)
    return pl.pallas_call(
        backward_kernel,
        grid=(regions,),
        in_specs=[
            pl.BlockSpec((feat, samples, rays), lambda t: (0, 0, t)),
            pl.BlockSpec((samples, rays), lambda t: (0, t)),
            pl.BlockSpec((1, rays), lambda t: (0, t)),
            whole(w2),
            whole(w3),
            pl.BlockSpec((1, 4, hidden, wide), lambda t: (t, 0, 0, 0)),
            pl.BlockSpec((1, PAD, wide), lambda t: (t, 0, 0)),
            pl.BlockSpec((1, rows, rays), lambda t: (t, 0, 0)),
        ],
        out_specs=pl.BlockSpec((blocks, 8, 128), lambda t: (0, 0, 0)),
        out_shape=jax.ShapeDtypeStruct((blocks, 8, 128), f32),
        scratch_shapes=[
            pltpu.VMEM((hidden, 3 * hidden), bf16),
            pltpu.VMEM((hidden, 256), bf16),
            pltpu.VMEM((feat, hidden), f32),
            pltpu.VMEM((hidden, hidden), f32),
            pltpu.VMEM((PAD, hidden), f32),
            pltpu.VMEM((3 * hidden, 128), f32),
        ],
        name="render_backward",
    )(features, spacing, counts, w2, w3, hiddens, raws, backs)


def remote(src, dst, sems, slot, device):
    return pltpu.make_async_remote_copy(
        src_ref=src,
        dst_ref=dst,
        send_sem=sems[0].at[slot],
        recv_sem=sems[1].at[slot],
        device_id=device,
        device_id_type=MESH,
    )


def compose_kernel(
    bits, channels,
    packed, target, rank_ref,
    pixels, back,
    *scratch,
):
    levels = len(bits[0])
    regions, rows, seg = packed.shape
    half = seg // len(bits)
    me = lax.axis_index("depth")
    sems = (scratch[-2], scratch[-1])
    got, work, notes = {}, {}, {}
    at = 0
    for h in range(len(bits)):
        for j in range(levels):
            got[h, j], work[h, j + 1], notes[h, j] = scratch[at : at + 3]
            at += 3
    slots = iter(range(10000))

    def my_bit(b):
        return lax.rem(me // (1 << b), 2)

    def partner(b):
        return {"depth": me + (1 - 2 * my_bit(b)) * (1 << b)}

    barrier = pltpu.get_barrier_semaphore()
    for b in range(levels):
        pl.semaphore_signal(barrier, inc=1, device_id=partner(b), device_id_type=MESH)
    pl.semaphore_wait(barrier, levels)

    rank = rank_ref[0:1, 0:1]

    def first(b):
        return lax.rem(lax.div(rank, jnp.full_like(rank, 1 << b)), jnp.full_like(rank, 2)) == 0

    def place(h, j, k, flip=False):
        total = 0
        for i in range(levels):
            b = bits[h][i]
            if i < j:
                bit = my_bit(b)
            else:
                bit = (k >> (levels - 1 - i)) & 1
            total = total + bit * (1 << b)
        return total

    def set_index(h, j, kk, mine):
        b = bits[h][j]
        bit = my_bit(b) if mine else 1 - my_bit(b)
        total = bit * (1 << b)
        for i in range(levels):
            c = bits[h][i]
            if i < j:
                total = total + my_bit(c) * (1 << c)
            elif i > j:
                total = total + ((kk >> (levels - 1 - i)) & 1) * (1 << c)
        return total

    def source(h, j, kk, mine):
        if j == 0:
            return packed.at[set_index(h, 0, kk, mine), :, pl.ds(h * half, half)]
        n2 = regions >> (j + 1)
        bit = my_bit(bits[h][j]) if mine else 1 - my_bit(bits[h][j])
        return work[h, j].at[bit * n2 + kk]

    def send(h, j):
        copies = []
        for kk in range(regions >> (j + 1)):
            copy = remote(
                source(h, j, kk, False), got[h, j].at[kk], sems, next(slots), partner(bits[h][j])
            )
            copy.start()
            copies.append(copy)
        return copies

    sent = {}
    for h in range(len(bits)):
        sent[h, 0] = send(h, 0)
    for j in range(levels):
        for h in range(len(bits)):
            ahead = first(bits[h][j])
            for kk, copy in enumerate(sent[h, j]):
                copy.wait()
                ours = source(h, j, kk, True)
                theirs = got[h, j].at[kk]
                mine, other = ours[...], theirs[...]
                mine_depth = mine[channels : channels + 1]
                other_depth = other[channels : channels + 1]
                mine_clear = jnp.where(ahead, 1.0, jnp.exp(-other_depth))
                other_clear = jnp.where(ahead, jnp.exp(-mine_depth), 1.0)
                work[h, j + 1][kk, 0:channels] = (
                    mine_clear * mine[0:channels] + other_clear * other[0:channels]
                )
                work[h, j + 1][kk, channels:rows] = mine[channels:rows] + other[channels:rows]
            if j + 1 < levels:
                sent[h, j + 1] = send(h, j + 1)

    flight = {}

    def send_misfit(h, j):
        copies = []
        for kk in range(regions >> (j + 1)):
            spot = back.at[set_index(h, j, kk, True), pl.ds(0, channels), pl.ds(h * half, half)]
            copy = remote(spot, spot, sems, next(slots), partner(bits[h][j]))
            copy.start()
            copies.append(copy)
        return copies

    for h in range(len(bits)):
        span = pl.ds(h * half, half)
        color = work[h, levels][0, 0:channels]
        pixels[:, span] = color
        back[me, 0:channels, span] = color - target[:, span]
        row = lax.broadcasted_iota(jnp.int32, (rows - channels, half), 0)
        back[me, channels:rows, span] = jnp.where(row == 0, 1.0, 0.0)
        flight[h] = send_misfit(h, levels - 1)
    for j in reversed(range(levels)):
        for h in range(len(bits)):
            span = pl.ds(h * half, half)
            b = bits[h][j]
            ahead = first(b)
            row = lax.broadcasted_iota(jnp.int32, (rows - channels, half), 0)
            copies = []
            for kk in range(regions >> (j + 1)):
                index = set_index(h, j, kk, True)
                mine = source(h, j, kk, True)[...]
                other = got[h, j][kk]
                misfit = back[index, 0:channels, span]
                state = back[index, channels:rows, span]
                passed, behind = state[0:1], state[1:2]
                mine_depth = mine[channels : channels + 1]
                other_depth = other[channels : channels + 1]
                hind = jnp.where(ahead, other[0:channels], mine[0:channels])
                later = passed * jnp.exp(-jnp.where(ahead, mine_depth, other_depth))
                glow = behind + later * jnp.sum(misfit * hind, axis=0, keepdims=True)
                mine_state = (jnp.where(ahead, passed, later), jnp.where(ahead, glow, behind))
                other_state = (jnp.where(ahead, later, passed), jnp.where(ahead, behind, glow))
                back[index, channels:rows, span] = jnp.where(row == 0, *mine_state)
                notes[h, j][kk] = jnp.where(row == 0, *other_state)
                spot = back.at[index, pl.ds(channels, rows - channels), span]
                copy = remote(notes[h, j].at[kk], spot, sems, next(slots), partner(b))
                copy.start()
                copies.append(copy)
            for copy in flight[h] + copies:
                copy.wait()
            if j:
                flight[h] = send_misfit(h, j - 1)


def compose(packed, target, rank):
    regions, rows, seg = packed.shape
    channels = target.shape[0]
    levels = regions.bit_length() - 1
    order = tuple(range(levels))
    bits = (order,) * min(2, seg // 128)
    half = seg // len(bits)
    scratch = []
    for _ in bits:
        for j in range(levels):
            n2 = regions >> (j + 1)
            scratch += [
                pltpu.VMEM((n2, rows, half), f32),
                pltpu.VMEM((n2, rows, half), f32),
                pltpu.VMEM((n2, rows - channels, half), f32),
            ]
    copies = len(bits) * 3 * (regions - 1)
    vmem = pl.BlockSpec(memory_space=pltpu.VMEM)
    return pl.pallas_call(
        functools.partial(compose_kernel, bits, channels),
        in_specs=[vmem] * 3,
        out_specs=[vmem] * 2,
        out_shape=[
            jax.ShapeDtypeStruct((channels, seg), f32),
            jax.ShapeDtypeStruct((regions, rows, seg), f32),
        ],
        scratch_shapes=scratch
        + [pltpu.SemaphoreType.DMA((copies,)), pltpu.SemaphoreType.DMA((copies,))],
        compiler_params=pltpu.CompilerParams(collective_id=0, has_side_effects=True),
        name="compose_swap",
    )(packed, target, rank)


def total_kernel(
    views, regions, feat, hidden, outs,
    grads, first_update, first_shift, second_update, second_shift, last_update, last_shift,
    total, *scratch,
):
    send_sems, recv_sems = scratch[-2], scratch[-1]
    sems = (send_sems, recv_sems)
    me = lax.axis_index("depth")
    view = lax.axis_index("view")
    levels = views.bit_length() - 1
    blocks = grads.shape[0]
    slots = iter(range(10000))

    def my_bit(b):
        return lax.rem(view // (1 << b), 2)

    def partner(b):
        return {"view": view + (1 - 2 * my_bit(b)) * (1 << b)}

    def peer(r):
        return {"depth": lax.rem(me + r, regions)}

    barrier = pltpu.get_barrier_semaphore()
    for b in range(levels):
        pl.semaphore_signal(barrier, inc=1, device_id=partner(b), device_id_type=MESH)
    for r in range(1, regions):
        pl.semaphore_signal(barrier, inc=1, device_id=peer(r), device_id_type=MESH)
    pl.semaphore_wait(barrier, levels + regions - 1)

    held = grads
    starts = [0]
    for b in range(levels):
        size = blocks >> (b + 1)
        copy = remote(
            held.at[pl.ds((1 - my_bit(b)) * size, size)],
            scratch[2 * b], sems, next(slots), partner(b),
        )
        copy.start()
        copy.wait()
        scratch[2 * b + 1][...] = held[pl.ds(my_bit(b) * size, size)] + scratch[2 * b][...]
        held = scratch[2 * b + 1]
        starts.append(starts[-1] + my_bit(b) * size)
    size = blocks // (views * regions)
    landing = scratch[2 * levels]
    copies = []
    for r in range(1, regions):
        to = lax.rem(me + r, regions)
        copy = remote(
            held.at[pl.ds(to * size, size)], landing.at[r - 1], sems, next(slots), peer(r)
        )
        copy.start()
        copies.append(copy)
    mine = held[pl.ds(me * size, size)]
    for copy in copies:
        copy.wait()
    for r in range(1, regions):
        mine = mine + landing[r - 1]
    spot = pl.ds(starts[-1] + me * size, size)
    total[spot] = mine
    copies = []
    for r in range(1, regions):
        copy = remote(total.at[spot], total.at[spot], sems, next(slots), peer(r))
        copy.start()
        copies.append(copy)
    for copy in copies:
        copy.wait()
    for b in reversed(range(levels)):
        size = blocks >> (b + 1)
        spot = pl.ds(starts[b + 1], size)
        copy = remote(total.at[spot], total.at[spot], sems, next(slots), partner(b))
        copy.start()
        copy.wait()

    def scaled(value, count):
        square = jnp.sum(jnp.sum(value * value, axis=0, keepdims=True), axis=1, keepdims=True)
        return value / jnp.sqrt(square / count + epsilon)

    at = 0
    wholes = []
    for rows in (hidden, feat, PAD):
        halves = []
        for _ in range(0, hidden, 128):
            halves.append(total[at : at + rows // 8].reshape(rows, 128))
            at += rows // 8
        wholes.append(jnp.concatenate(halves, axis=1))
    second_update[...] = scaled(wholes[0], hidden * hidden)
    first_update[...] = scaled(wholes[1], feat * hidden)
    last = scaled(wholes[2], hidden * outs)
    last = jnp.concatenate([last, jnp.zeros((128 - PAD, hidden), f32)], axis=0).T
    last_update[...] = last[:, 0:outs]
    rows = total[at]
    first_shift[...] = scaled(jnp.concatenate([rows[0:1], rows[1:2]], axis=1), hidden)
    second_shift[...] = scaled(jnp.concatenate([rows[2:3], rows[3:4]], axis=1), hidden)
    last_shift[...] = scaled(rows[4:5], outs)[:, 0:outs]


def total_gradients(grads, views, regions, feat, hidden, outs):
    blocks = grads.shape[0]
    levels = views.bit_length() - 1
    scratch = [pltpu.VMEM((blocks, 8, 128), f32)]
    for b in range(levels):
        size = blocks >> (b + 1)
        scratch += [pltpu.VMEM((size, 8, 128), f32)] * 2
    size = blocks // (views * regions)
    scratch.append(pltpu.VMEM((regions - 1, size, 8, 128), f32))
    copies = 2 * (levels + regions - 1)
    vmem = pl.BlockSpec(memory_space=pltpu.VMEM)
    shapes = [(feat, hidden), (1, hidden), (hidden, hidden), (1, hidden), (hidden, outs), (1, outs)]
    return pl.pallas_call(
        functools.partial(total_kernel, views, regions, feat, hidden, outs),
        in_specs=[vmem],
        out_specs=[vmem] * 6,
        out_shape=[jax.ShapeDtypeStruct(shape, f32) for shape in shapes],
        scratch_shapes=scratch
        + [pltpu.SemaphoreType.DMA((copies,)), pltpu.SemaphoreType.DMA((copies,))],
        compiler_params=pltpu.CompilerParams(collective_id=1, has_side_effects=True),
        name="gradient_total",
    )(grads)


def local(
    features, spacing, counts, depth_rank, target,
    first_weight, first_bias, second_weight, second_bias, last_weight, last_bias,
):
    regions = lax.axis_size("depth")
    views = lax.axis_size("view")
    feat, hidden = first_weight.shape
    outs = last_weight.shape[1]
    feats, gaps, live = features[0, 0], spacing[0, 0], counts[0]
    weights = (
        first_weight, first_bias[None], second_weight, second_bias[None],
        last_weight, last_bias[None],
    )
    packed, hiddens, raws = forward(feats, gaps, live, weights, regions)
    pixels, backs = compose(packed, target[0], depth_rank)
    blocks = block_count(feat, hidden, views * regions)
    grads = backward(
        feats, gaps, live, second_weight, last_weight, hiddens, raws, backs, blocks
    )
    results = total_gradients(grads, views, regions, feat, hidden, outs)
    return (
        pixels[None], results[0], results[1][0], results[2], results[3][0], results[4], results[5][0],
    )


def solution(mesh):
    return jax.shard_map(
        local,
        mesh=mesh,
        in_specs=(
            P("view", "depth", None, None, None),
            P("view", "depth", None, None),
            P("view", "depth", None),
            P("view", "depth"),
            P("view", None, "depth"),
            P(), P(), P(), P(), P(), P(),
        ),
        out_specs=(P("view", None, "depth"), P(), P(), P(), P(), P(), P()),
        check_vma=False,
    )
```

```python
import functools

import jax
import jax.numpy as jnp
from jax import lax
from jax.experimental import pallas as pl
from jax.experimental.pallas import tpu as pltpu
from jax.sharding import PartitionSpec as P

epsilon = 1e-05
PAD = 80
MESH = pl.DeviceIdType.MESH
f32 = jnp.float32
bf16 = jnp.bfloat16


def split(value):
    high = value.astype(bf16)
    low = (value - high.astype(f32)).astype(bf16)
    return high, low


def mm(left, right):
    return lax.dot_general(left, right, (((1,), (0,)), ((), ())), preferred_element_type=f32)


def mm_nt(left, right):
    return lax.dot_general(left, right, (((1,), (1,)), ((), ())), preferred_element_type=f32)


def opticals(raw, channels, spacing, counts, samples, rays):
    out = []
    for s in range(samples):
        logit = raw[channels : channels + 1, s * rays : (s + 1) * rays]
        density = jnp.maximum(logit, 0.0) + jnp.log1p(jnp.exp(-jnp.abs(logit)))
        length = jnp.where(s < counts, spacing[s], 0.0)
        out.append((logit, density * length, length))
    return out


def remote(src, dst, sems, slot, device):
    return pltpu.make_async_remote_copy(
        src_ref=src,
        dst_ref=dst,
        send_sem=sems[0].at[slot],
        recv_sem=sems[1].at[slot],
        device_id=device,
        device_id_type=MESH,
    )


def lanes(value):
    total = value[:, 0:128]
    for lane in range(128, value.shape[1], 128):
        total = total + value[:, lane : lane + 128]
    return total


def block_count(feat, hidden, devices):
    blocks = (hidden + feat + PAD) // 8 * (hidden // 128) + 1
    return -(-blocks // devices) * devices


def prepare(feat, w1_ref, b1_ref, w2_ref, b2_ref, w3_ref, b3_ref, w1s, w2f, w2b, w3f, w3b, cols):
    hidden = w2_ref.shape[0]
    outs = w3_ref.shape[0]
    high, low = split(w1_ref[...])
    bias = b1_ref[...]
    bias_a = bias.astype(bf16).astype(f32)
    bias_b = (bias - bias_a).astype(bf16).astype(f32)
    cols[...] = jnp.zeros_like(cols)
    cols[0:feat, :] = high.astype(f32)
    cols[feat : 2 * feat, :] = high.astype(f32)
    cols[2 * feat : 3 * feat, :] = low.astype(f32)
    cols[3 * feat : 3 * feat + 1, :] = bias_a
    cols[3 * feat + 1 : 3 * feat + 2, :] = bias_b
    cols[3 * feat + 2 : 3 * feat + 3, :] = bias - bias_a - bias_b
    cols[3 * feat + 3 : 3 * feat + 4, :] = b2_ref[...]
    cols[3 * feat + 4 : 3 * feat + 5, 0:outs] = b3_ref[...]
    turned = cols[0:128, :].T
    w1s[...] = turned.astype(bf16)
    cols[:, 0:128] = turned
    for stack, weight in ((w2f, w2_ref[...].T), (w2b, w2_ref[...])):
        high, low = split(weight)
        stack[:, 0:hidden] = high
        stack[:, hidden : 2 * hidden] = high
        stack[:, 2 * hidden : 3 * hidden] = low
    tall = jnp.concatenate([w3_ref[...], jnp.zeros((PAD - outs, hidden), f32)], axis=0)
    high, low = split(tall)
    w3f[0:PAD, :] = high
    w3f[PAD : 2 * PAD, :] = low
    high = high.astype(f32)
    stack = jnp.concatenate(
        [high, high, tall - high, jnp.zeros((256 - 3 * PAD, hidden), f32)], axis=0
    )
    w3b[...] = stack.T.astype(bf16)


def forward_tile(feat, channels, x, spacing, counts, w1s, w2f, w3f, cols, keep_x, keep_h, keep_raw):
    samples = len(spacing)
    rays = spacing[0].shape[1]
    xh, xl = split(x)
    keep_x[0] = xh
    keep_x[1] = xl
    rows = lax.broadcasted_iota(jnp.int32, x.shape, 0)
    ones = jnp.where(rows < 3, 1.0, 0.0).astype(bf16)
    z1 = mm(w1s[...], jnp.concatenate([xh, xl, xh, ones], axis=0))
    h1h, h1l = split(jnp.maximum(z1, 0.0))
    keep_h[0] = h1h
    keep_h[1] = h1l
    z2 = mm(w2f[...], jnp.concatenate([h1h, h1l, h1h], axis=0))
    z2 = z2 + cols[:, 3 * feat + 3 : 3 * feat + 4]
    h2h, h2l = split(jnp.maximum(z2, 0.0))
    keep_h[2] = h2h
    keep_h[3] = h2l
    both = mm(w3f[...], h2h)
    raw = both[0:PAD] + both[PAD:] + mm(w3f[0:PAD, :], h2l)
    raw = raw + cols[0:PAD, 3 * feat + 4 : 3 * feat + 5]
    keep_raw[...] = raw
    before = None
    color = None
    parts = opticals(raw, channels, spacing, counts, samples, rays)
    for s, (_, optical, _) in enumerate(parts):
        weight = 1.0 - jnp.exp(-optical)
        if s:
            weight = jnp.exp(-before) * weight
        shade = weight * jax.nn.sigmoid(raw[0:channels, s * rays : (s + 1) * rays])
        color = shade if s == 0 else color + shade
        before = optical if s == 0 else before + optical
    return color, before


def backward_tile(
    channels, raw, misfit, state, spacing, counts, keep_x, keep_h, w2b, w3b,
    acc1, acc2, acc3, bias,
):
    samples = len(spacing)
    rays = spacing[0].shape[1]
    hidden = w2b.shape[0]
    feat = keep_x.shape[1]
    passed = state[0:1]
    parts = opticals(raw, channels, spacing, counts, samples, rays)
    befores, before = [], None
    for s in range(samples):
        befores.append(before)
        before = parts[s][1] if s == 0 else before + parts[s][1]
    tail = -state[1:2]
    pieces = [None] * samples
    for s in reversed(range(samples)):
        logit, optical, length = parts[s]
        gone = jnp.exp(-optical)
        ahead = 1.0 if s == 0 else jnp.exp(-befores[s])
        weight = ahead * (1.0 - gone)
        color = jax.nn.sigmoid(raw[0:channels, s * rays : (s + 1) * rays])
        weight_grad = passed * jnp.sum(misfit * color, axis=0, keepdims=True)
        optical_grad = weight_grad * (ahead * gone) + tail
        tail = tail - weight_grad * weight
        color_grad = (weight * passed) * misfit * (color * (1.0 - color))
        logit_grad = optical_grad * length * jax.nn.sigmoid(logit)
        row = lax.broadcasted_iota(jnp.int32, (PAD - channels, rays), 0)
        rest = jnp.where(row == 0, jnp.broadcast_to(logit_grad, row.shape), 0.0)
        pieces[s] = jnp.concatenate([color_grad, rest], axis=0)
    draw = jnp.concatenate(pieces, axis=1)
    bias[2 * hidden : 2 * hidden + PAD, :] += lanes(draw)
    dh, dl = split(draw)
    h2h = keep_h[2]
    h2l = keep_h[3]
    both = mm_nt(jnp.concatenate([dh, dl], axis=0), h2h)
    acc3[...] += both[0:PAD] + both[PAD:] + mm_nt(dh, h2l)
    zero = jnp.zeros((256 - 3 * PAD, draw.shape[1]), bf16)
    dh2 = mm(w3b[...], jnp.concatenate([dh, dl, dh, zero], axis=0))
    dz2 = jnp.where(h2h > 0, dh2, 0.0)
    bias[hidden : 2 * hidden, :] += lanes(dz2)
    zh, zl = split(dz2)
    h1h = keep_h[0]
    h1l = keep_h[1]
    acc2[...] += mm_nt(h1h, zh) + mm_nt(h1l, zh) + mm_nt(h1h, zl)
    dh1 = mm(w2b[...], jnp.concatenate([zh, zl, zh], axis=0))
    dz1 = jnp.where(h1h > 0, dh1, 0.0)
    bias[0:hidden, :] += lanes(dz1)
    xh = keep_x[0]
    xl = keep_x[1]
    zh, zl = split(dz1)
    both = mm_nt(jnp.concatenate([xh, xl], axis=0), zh)
    acc1[...] += both[0:feat] + both[feat:] + mm_nt(xh, zl)


def step_kernel(
    views, regions,
    feats, spacing, counts, target, rank_ref, w1, b1, w2, b2, w3, b3,
    pixels, total,
    w1s, w2f, w2b, w3f, w3b, cols, keep_x, keep_h, keep_raw, back, grads,
    acc1, acc2, acc3, bias, fsend, frecv, msend, mrecv, nsend, nrecv, gsend, grecv,
    *scratch,
):
    samples, feat, rays = feats.shape
    channels, seg = target.shape
    levels = regions.bit_length() - 1
    rows = back.shape[1]
    hidden = w2.shape[0]
    me = lax.axis_index("depth")
    view = lax.axis_index("view")
    vlevels = views.bit_length() - 1
    work = scratch[0 : levels + 1]
    got = scratch[levels + 1 : 2 * levels + 1]
    notes = scratch[2 * levels + 1 : 3 * levels + 1]
    sums = scratch[3 * levels + 1 :]

    def bit_of(value, b):
        return lax.rem(value // (1 << b), 2)

    def partner(b):
        return {"depth": me + (1 - 2 * bit_of(me, b)) * (1 << b)}

    def view_partner(b):
        return {"view": view + (1 - 2 * bit_of(view, b)) * (1 << b)}

    def peer(r):
        return {"depth": lax.rem(me + r, regions)}

    barrier = pltpu.get_barrier_semaphore()
    for b in range(vlevels):
        pl.semaphore_signal(barrier, inc=1, device_id=view_partner(b), device_id_type=MESH)
    for r in range(1, regions):
        pl.semaphore_signal(barrier, inc=1, device_id=peer(r), device_id_type=MESH)

    prepare(feat, w1, b1, w2, b2, w3, b3, w1s, w2f, w2b, w3f, w3b, cols)
    pl.semaphore_wait(barrier, vlevels + regions - 1)

    def span_of(k):
        where = 0
        for b in range(levels):
            where = where + lax.rem(bit_of(me, b) + bit_of(k, levels - 1 - b), 2) * (1 << b)
        return pl.ds(pl.multiple_of(where * seg, seg), seg)

    rank = rank_ref[0:1, 0:1]

    def first(b):
        return lax.rem(lax.div(rank, jnp.full_like(rank, 1 << b)), jnp.full_like(rank, 2)) == 0

    def color_copy(j, kk):
        n2 = regions >> (j + 1)
        return remote(work[j].at[n2 + kk], got[j].at[kk], (fsend, frecv), n2 + kk, partner(j))

    def misfit_copy(j, kk):
        n2 = regions >> (j + 1)
        part = pl.ds(0, channels)
        return remote(
            back.at[kk, part], back.at[n2 + kk, part], (msend, mrecv), n2 + kk, partner(j)
        )

    def note_copy(j, kk):
        n2 = regions >> (j + 1)
        return remote(
            notes[j].at[kk], back.at[n2 + kk, pl.ds(channels, rows - channels)],
            (nsend, nrecv), n2 + kk, partner(j),
        )

    def gather_x(span):
        return jnp.concatenate([feats[s, :, span] for s in range(samples)], axis=1)

    def forward_step(i, carry):
        k = regions - 1 - i
        span = span_of(k)
        color, depth = forward_tile(
            feat, channels, gather_x(span), [spacing[s, :, span] for s in range(samples)], counts[:, span],
            w1s, w2f, w3f, cols, keep_x.at[k], keep_h.at[k], keep_raw.at[k],
        )
        work[0][k, 0:channels] = color
        work[0][k, channels:rows] = jnp.broadcast_to(depth, (rows - channels, seg))
        for j in range(levels):
            n2 = regions >> (j + 1)

            @pl.when((k >= n2) & (k < 2 * n2))
            def _():
                color_copy(j, k - n2).start()

            @pl.when(k < n2)
            def _():
                color_copy(j, k).wait_recv()
                ahead = first(j)
                mine, other = work[j][k], got[j][k]
                mine_depth = mine[channels : channels + 1]
                other_depth = other[channels : channels + 1]
                mine_clear = jnp.where(ahead, 1.0, jnp.exp(-other_depth))
                other_clear = jnp.where(ahead, jnp.exp(-mine_depth), 1.0)
                work[j + 1][k, 0:channels] = (
                    mine_clear * mine[0:channels] + other_clear * other[0:channels]
                )
                work[j + 1][k, channels:rows] = mine[channels:rows] + other[channels:rows]

        return carry

    lax.fori_loop(0, regions, forward_step, 0)
    color = work[levels][0, 0:channels]
    pixels[...] = color
    row = lax.broadcasted_iota(jnp.int32, (rows - channels, seg), 0)
    back[0, 0:channels] = color - target[...]
    back[0, channels:rows] = jnp.where(row == 0, 1.0, 0.0)
    for acc in (acc1, acc2, acc3, bias):
        acc[...] = jnp.zeros_like(acc)
    order = sorted(range(regions), key=lambda k: (bin(k).count("1"), -k))

    def backward_step(i, carry):
        k = 0
        for at, value in enumerate(order):
            k = k + jnp.where(i == at, value, 0)
        for j in range(levels):
            n2 = regions >> (j + 1)

            @pl.when((k >= n2) & (k < 2 * n2))
            def _():
                misfit_copy(j, k - n2).wait_recv()
                note_copy(j, k - n2).wait_recv()

        for j in reversed(range(levels)):
            n2 = regions >> (j + 1)

            @pl.when(k < n2)
            def _():
                misfit_copy(j, k).start()

        for j in reversed(range(levels)):
            n2 = regions >> (j + 1)

            @pl.when(k < n2)
            def _():
                ahead = first(j)
                mine, other = work[j][k], got[j][k]
                misfit = back[k, 0:channels]
                state = back[k, channels:rows]
                passed, behind = state[0:1], state[1:2]
                mine_depth = mine[channels : channels + 1]
                other_depth = other[channels : channels + 1]
                hind = jnp.where(ahead, other[0:channels], mine[0:channels])
                later = passed * jnp.exp(-jnp.where(ahead, mine_depth, other_depth))
                glow = behind + later * jnp.sum(misfit * hind, axis=0, keepdims=True)
                mine_state = (jnp.where(ahead, passed, later), jnp.where(ahead, glow, behind))
                other_state = (jnp.where(ahead, later, passed), jnp.where(ahead, behind, glow))
                notes[j][k] = jnp.where(row == 0, *other_state)
                note_copy(j, k).start()
                back[k, channels:rows] = jnp.where(row == 0, *mine_state)

        span = span_of(k)
        backward_tile(
            channels, keep_raw[k], back[k, 0:channels], back[k, channels:rows],
            [spacing[s, :, span] for s in range(samples)], counts[:, span], keep_x.at[k], keep_h.at[k], w2b, w3b,
            acc1, acc2, acc3, bias,
        )
        return carry

    lax.fori_loop(0, regions, backward_step, 0)
    for j in range(levels):
        n2 = regions >> (j + 1)
        for kk in range(n2):
            color_copy(j, kk).wait_send()
            misfit_copy(j, kk).wait_send()
            note_copy(j, kk).wait_send()

    at = 0
    for acc in (acc2, acc1, acc3):
        blocks = acc.shape[0] // 8
        for lane in range(0, hidden, 128):
            grads[at : at + blocks] = acc[:, lane : lane + 128].reshape(blocks, 8, 128)
            at += blocks
    grads[at:] = jnp.zeros((grads.shape[0] - at, 8, 128), f32)
    added = jnp.sum(bias[...].T, axis=0, keepdims=True)
    for lane in range(5):
        grads[at, lane : lane + 1, :] = added[:, lane * 128 : (lane + 1) * 128]

    blocks = grads.shape[0]
    slots = iter(range(10000))
    sems = (gsend, grecv)
    held = grads
    starts = [0]
    for b in range(vlevels):
        size = blocks >> (b + 1)
        copy = remote(
            held.at[pl.ds((1 - bit_of(view, b)) * size, size)],
            sums[2 * b], sems, next(slots), view_partner(b),
        )
        copy.start()
        copy.wait()
        sums[2 * b + 1][...] = held[pl.ds(bit_of(view, b) * size, size)] + sums[2 * b][...]
        held = sums[2 * b + 1]
        starts.append(starts[-1] + bit_of(view, b) * size)
    size = blocks // (views * regions)
    landing = sums[2 * vlevels]
    copies = []
    for r in range(1, regions):
        to = lax.rem(me + r, regions)
        copy = remote(
            held.at[pl.ds(to * size, size)], landing.at[r - 1], sems, next(slots), peer(r)
        )
        copy.start()
        copies.append(copy)
    mine = held[pl.ds(me * size, size)]
    for copy in copies:
        copy.wait()
    for r in range(1, regions):
        mine = mine + landing[r - 1]
    spot = pl.ds(starts[-1] + me * size, size)
    total[spot] = mine
    copies = []
    for r in range(1, regions):
        copy = remote(total.at[spot], total.at[spot], sems, next(slots), peer(r))
        copy.start()
        copies.append(copy)
    for copy in copies:
        copy.wait()
    for b in reversed(range(vlevels)):
        size = blocks >> (b + 1)
        spot = pl.ds(starts[b + 1], size)
        copy = remote(total.at[spot], total.at[spot], sems, next(slots), view_partner(b))
        copy.start()
        copy.wait()


def whole_step(views, regions, feats, spacing, counts, target, rank, weights):
    samples, feat, rays = feats.shape
    channels, seg = target.shape
    hidden = weights[2].shape[0]
    levels = regions.bit_length() - 1
    vlevels = views.bit_length() - 1
    rows = channels + 8
    wide = samples * seg
    blocks = block_count(feat, hidden, views * regions)
    size = blocks // (views * regions)
    scratch = [
        pltpu.VMEM((hidden, 128), bf16),
        pltpu.VMEM((hidden, 3 * hidden), bf16),
        pltpu.VMEM((hidden, 3 * hidden), bf16),
        pltpu.VMEM((2 * PAD, hidden), bf16),
        pltpu.VMEM((hidden, 256), bf16),
        pltpu.VMEM((hidden, hidden), f32),
        pltpu.VMEM((regions, 2, feat, wide), bf16),
        pltpu.VMEM((regions, 4, hidden, wide), bf16),
        pltpu.VMEM((regions, PAD, wide), f32),
        pltpu.VMEM((regions, rows, seg), f32),
        pltpu.VMEM((blocks, 8, 128), f32),
        pltpu.VMEM((feat, hidden), f32),
        pltpu.VMEM((hidden, hidden), f32),
        pltpu.VMEM((PAD, hidden), f32),
        pltpu.VMEM((3 * hidden, 128), f32),
    ]
    scratch += [pltpu.SemaphoreType.DMA((regions,))] * 6
    scratch += [pltpu.SemaphoreType.DMA((2 * (vlevels + regions - 1),))] * 2
    scratch += [pltpu.VMEM((regions >> j, rows, seg), f32) for j in range(levels + 1)]
    scratch += [pltpu.VMEM((regions >> (j + 1), rows, seg), f32) for j in range(levels)]
    scratch += [pltpu.VMEM((regions >> (j + 1), 8, seg), f32) for j in range(levels)]
    for b in range(vlevels):
        scratch += [pltpu.VMEM((blocks >> (b + 1), 8, 128), f32)] * 2
    scratch.append(pltpu.VMEM((regions - 1, size, 8, 128), f32))
    vmem = pl.BlockSpec(memory_space=pltpu.VMEM)
    return pl.pallas_call(
        functools.partial(step_kernel, views, regions),
        in_specs=[vmem] * 11,
        out_specs=[vmem] * 2,
        out_shape=[
            jax.ShapeDtypeStruct((channels, seg), f32),
            jax.ShapeDtypeStruct((blocks, 8, 128), f32),
        ],
        scratch_shapes=scratch,
        compiler_params=pltpu.CompilerParams(
            collective_id=0, has_side_effects=True, vmem_limit_bytes=66000000
        ),
        name="whole_step",
    )(feats, spacing, counts, target, rank, *weights)


def finish_kernel(
    feat, hidden, outs,
    pixels_in, total,
    pixels, first_update, first_shift, second_update, second_shift, last_update, last_shift,
):
    def scaled(value, count):
        square = jnp.sum(jnp.sum(value * value, axis=0, keepdims=True), axis=1, keepdims=True)
        return value / jnp.sqrt(square / count + epsilon)

    pixels[...] = pixels_in[...]
    at = 0
    wholes = []
    for rows in (hidden, feat, PAD):
        halves = []
        for _ in range(0, hidden, 128):
            halves.append(total[at : at + rows // 8].reshape(rows, 128))
            at += rows // 8
        wholes.append(jnp.concatenate(halves, axis=1))
    second_update[...] = scaled(wholes[0], hidden * hidden)
    first_update[...] = scaled(wholes[1], feat * hidden)
    last_update[...] = scaled(wholes[2], hidden * outs)[0:outs]
    rows = total[at]
    first_shift[...] = scaled(jnp.concatenate([rows[0:1], rows[1:2]], axis=1), hidden)
    second_shift[...] = scaled(jnp.concatenate([rows[2:3], rows[3:4]], axis=1), hidden)
    last_shift[...] = scaled(rows[4:5], outs)[:, 0:outs]


def finish(pixels, total, feat, hidden, outs):
    vmem = pl.BlockSpec(memory_space=pltpu.VMEM)
    shapes = [
        pixels.shape, (feat, hidden), (1, hidden), (hidden, hidden), (1, hidden),
        (outs, hidden), (1, outs),
    ]
    return pl.pallas_call(
        functools.partial(finish_kernel, feat, hidden, outs),
        in_specs=[vmem] * 2,
        out_specs=[vmem] * len(shapes),
        out_shape=[jax.ShapeDtypeStruct(shape, f32) for shape in shapes],
        name="normalize_all",
    )(pixels, total)


def local(
    features, spacing, counts, depth_rank, target,
    first_weight, first_bias, second_weight, second_bias, last_weight, last_bias,
):
    regions = lax.axis_size("depth")
    views = lax.axis_size("view")
    feat, hidden = first_weight.shape
    outs = last_weight.shape[1]
    feats, gaps, live = jnp.transpose(features[0, 0], (1, 0, 2)), jnp.transpose(spacing[0], (1, 0, 2)), counts[0]
    weights = (
        first_weight, first_bias[None], second_weight, second_bias[None],
        last_weight.T, last_bias[None],
    )
    pixels, total = whole_step(views, regions, feats, gaps, live, target[0], depth_rank, weights)
    results = finish(pixels, total, feat, hidden, outs)
    return (
        results[0][None], results[1], results[2][0], results[3], results[4][0],
        results[5].T, results[6][0],
    )


def solution(mesh):
    return jax.shard_map(
        local,
        mesh=mesh,
        in_specs=(
            P("view", "depth", None, None, None),
            P("view", "depth", None, None),
            P("view", "depth", None),
            P("view", "depth"),
            P("view", None, "depth"),
            P(), P(), P(), P(), P(), P(),
        ),
        out_specs=(P("view", None, "depth"), P(), P(), P(), P(), P(), P()),
        check_vma=False,
    )
```

```python
import functools

import jax
import jax.numpy as jnp
from jax import lax
from jax.experimental import pallas as pl
from jax.experimental.pallas import tpu as pltpu
from jax.sharding import PartitionSpec as P

epsilon = 1e-05
PAD = 80
MESH = pl.DeviceIdType.MESH
f32 = jnp.float32
bf16 = jnp.bfloat16


def split(value):
    high = value.astype(bf16)
    low = (value - high.astype(f32)).astype(bf16)
    return high, low


def mm(left, right):
    return lax.dot_general(left, right, (((1,), (0,)), ((), ())), preferred_element_type=f32)


def mm_nt(left, right):
    return lax.dot_general(left, right, (((1,), (1,)), ((), ())), preferred_element_type=f32)


def opticals(raw, channels, spacing, counts, samples, rays):
    out = []
    for s in range(samples):
        logit = raw[channels : channels + 1, s * rays : (s + 1) * rays]
        density = jnp.maximum(logit, 0.0) + jnp.log1p(jnp.exp(-jnp.abs(logit)))
        length = jnp.where(s < counts, spacing[s], 0.0)
        out.append((logit, density * length, length))
    return out


def remote(src, dst, sems, slot, device):
    return pltpu.make_async_remote_copy(
        src_ref=src,
        dst_ref=dst,
        send_sem=sems[0].at[slot],
        recv_sem=sems[1].at[slot],
        device_id=device,
        device_id_type=MESH,
    )


def lanes(value):
    total = value[:, 0:128]
    for lane in range(128, value.shape[1], 128):
        total = total + value[:, lane : lane + 128]
    return total


def round_up(blocks, devices):
    return -(-blocks // devices) * devices


def block_counts(feat, hidden, devices):
    across = hidden // 128
    late = feat // 8 * across + 1
    early = (hidden + PAD) // 8 * across + 1
    return round_up(early, devices), round_up(late, devices)


def fill(grads, accs, rows):
    at = 0
    for acc in accs:
        blocks = acc.shape[0] // 8
        for lane in range(0, acc.shape[1], 128):
            grads[at : at + blocks] = acc[:, lane : lane + 128].reshape(blocks, 8, 128)
            at += blocks
    grads[at:] = jnp.zeros((grads.shape[0] - at, 8, 128), f32)
    added = jnp.sum(rows.T, axis=0, keepdims=True)
    for i, lane in enumerate(range(0, rows.shape[0], 128)):
        grads[at, i : i + 1, :] = added[:, lane : lane + 128]


def total_stages(views, regions, grads, total, sums, sems):
    me = lax.axis_index("depth")
    view = lax.axis_index("view")
    vlevels = views.bit_length() - 1
    blocks = grads.shape[0]
    small = blocks // (views * regions)
    landing = sums[2 * vlevels]

    def bit_of(b):
        return lax.rem(view // (1 << b), 2)

    def view_partner(b):
        return {"view": view + (1 - 2 * bit_of(b)) * (1 << b)}

    def peer(r):
        return {"depth": lax.rem(me + r, regions)}

    def held(b):
        return grads if b == 0 else sums[2 * b - 1]

    def base(b):
        start = 0
        for c in range(b):
            start = start + bit_of(c) * (blocks >> (c + 1))
        return start

    def scatter_view(b):
        size = blocks >> (b + 1)
        part = pl.ds((1 - bit_of(b)) * size, size)
        return [remote(held(b).at[part], sums[2 * b], sems, b, view_partner(b))]

    def add_view(b):
        size = blocks >> (b + 1)
        sums[2 * b + 1][...] = held(b)[pl.ds(bit_of(b) * size, size)] + sums[2 * b][...]

    def scatter_depth():
        return [
            remote(
                held(vlevels).at[pl.ds(lax.rem(me + r, regions) * small, small)],
                landing.at[r - 1], sems, vlevels + r - 1, peer(r),
            )
            for r in range(1, regions)
        ]

    def spot():
        return pl.ds(base(vlevels) + me * small, small)

    def add_depth():
        mine = held(vlevels)[pl.ds(me * small, small)]
        for r in range(1, regions):
            mine = mine + landing[r - 1]
        total[spot()] = mine

    def gather_depth():
        part = total.at[spot()]
        first = vlevels + regions - 1
        return [remote(part, part, sems, first + r - 1, peer(r)) for r in range(1, regions)]

    def gather_view(b):
        part = total.at[pl.ds(base(b + 1), blocks >> (b + 1))]
        slot = vlevels + 2 * (regions - 1) + b
        return [remote(part, part, sems, slot, view_partner(b))]

    moves = [
        (functools.partial(scatter_view, b), functools.partial(add_view, b))
        for b in range(vlevels)
    ]
    moves.append((scatter_depth, add_depth))
    moves.append((gather_depth, None))
    moves += [(functools.partial(gather_view, b), None) for b in reversed(range(vlevels))]

    def stage(n):
        if n > 0:
            copies, after = moves[n - 1]
            for copy in copies():
                copy.wait()
            if after is not None:
                after()
        if n < len(moves):
            for copy in moves[n][0]():
                copy.start()

    return [functools.partial(stage, n) for n in range(len(moves) + 1)]


def prepare(feat, w1_ref, b1_ref, w2_ref, b2_ref, w3_ref, b3_ref, w1s, w2f, w2b, w3f, w3b, cols):
    hidden = w2_ref.shape[0]
    outs = w3_ref.shape[0]
    high, low = split(w1_ref[...])
    bias = b1_ref[...]
    bias_a = bias.astype(bf16).astype(f32)
    bias_b = (bias - bias_a).astype(bf16).astype(f32)
    cols[...] = jnp.zeros_like(cols)
    cols[0:feat, :] = high.astype(f32)
    cols[feat : 2 * feat, :] = high.astype(f32)
    cols[2 * feat : 3 * feat, :] = low.astype(f32)
    cols[3 * feat : 3 * feat + 1, :] = bias_a
    cols[3 * feat + 1 : 3 * feat + 2, :] = bias_b
    cols[3 * feat + 2 : 3 * feat + 3, :] = bias - bias_a - bias_b
    cols[3 * feat + 3 : 3 * feat + 4, :] = b2_ref[...]
    cols[3 * feat + 4 : 3 * feat + 5, 0:outs] = b3_ref[...]
    turned = cols[0:128, :].T
    w1s[...] = turned.astype(bf16)
    cols[:, 0:128] = turned
    for stack, weight in ((w2f, w2_ref[...].T), (w2b, w2_ref[...])):
        high, low = split(weight)
        stack[:, 0:hidden] = high
        stack[:, hidden : 2 * hidden] = high
        stack[:, 2 * hidden : 3 * hidden] = low
    tall = jnp.concatenate([w3_ref[...], jnp.zeros((PAD - outs, hidden), f32)], axis=0)
    high, low = split(tall)
    w3f[0:PAD, :] = high
    w3f[PAD : 2 * PAD, :] = low
    high = high.astype(f32)
    stack = jnp.concatenate(
        [high, high, tall - high, jnp.zeros((256 - 3 * PAD, hidden), f32)], axis=0
    )
    w3b[...] = stack.T.astype(bf16)


def forward_tile(feat, channels, x, spacing, counts, w1s, w2f, w3f, cols, keep_x, keep_h, keep_raw):
    samples = len(spacing)
    rays = spacing[0].shape[1]
    xh, xl = split(x)
    keep_x[0] = xh
    keep_x[1] = xl
    rows = lax.broadcasted_iota(jnp.int32, x.shape, 0)
    ones = jnp.where(rows < 3, 1.0, 0.0).astype(bf16)
    z1 = mm(w1s[...], jnp.concatenate([xh, xl, xh, ones], axis=0))
    h1h, h1l = split(jnp.maximum(z1, 0.0))
    keep_h[0] = h1h
    keep_h[1] = h1l
    z2 = mm(w2f[...], jnp.concatenate([h1h, h1l, h1h], axis=0))
    z2 = z2 + cols[:, 3 * feat + 3 : 3 * feat + 4]
    h2h, h2l = split(jnp.maximum(z2, 0.0))
    keep_h[2] = h2h
    keep_h[3] = h2l
    both = mm(w3f[...], h2h)
    raw = both[0:PAD] + both[PAD:] + mm(w3f[0:PAD, :], h2l)
    raw = raw + cols[0:PAD, 3 * feat + 4 : 3 * feat + 5]
    keep_raw[...] = raw
    before = None
    color = None
    parts = opticals(raw, channels, spacing, counts, samples, rays)
    for s, (_, optical, _) in enumerate(parts):
        weight = 1.0 - jnp.exp(-optical)
        if s:
            weight = jnp.exp(-before) * weight
        shade = weight * jax.nn.sigmoid(raw[0:channels, s * rays : (s + 1) * rays])
        color = shade if s == 0 else color + shade
        before = optical if s == 0 else before + optical
    return color, before


def backward_tile(
    channels, raw, misfit, state, spacing, counts, keep_h, w3b, acc2, acc3, bias,
):
    samples = len(spacing)
    rays = spacing[0].shape[1]
    hidden = w3b.shape[0]
    passed = state[0:1]
    parts = opticals(raw, channels, spacing, counts, samples, rays)
    befores, before = [], None
    for s in range(samples):
        befores.append(before)
        before = parts[s][1] if s == 0 else before + parts[s][1]
    tail = -state[1:2]
    pieces = [None] * samples
    for s in reversed(range(samples)):
        logit, optical, length = parts[s]
        gone = jnp.exp(-optical)
        ahead = 1.0 if s == 0 else jnp.exp(-befores[s])
        weight = ahead * (1.0 - gone)
        color = jax.nn.sigmoid(raw[0:channels, s * rays : (s + 1) * rays])
        weight_grad = passed * jnp.sum(misfit * color, axis=0, keepdims=True)
        optical_grad = weight_grad * (ahead * gone) + tail
        tail = tail - weight_grad * weight
        color_grad = (weight * passed) * misfit * (color * (1.0 - color))
        logit_grad = optical_grad * length * jax.nn.sigmoid(logit)
        row = lax.broadcasted_iota(jnp.int32, (PAD - channels, rays), 0)
        rest = jnp.where(row == 0, jnp.broadcast_to(logit_grad, row.shape), 0.0)
        pieces[s] = jnp.concatenate([color_grad, rest], axis=0)
    draw = jnp.concatenate(pieces, axis=1)
    bias[2 * hidden : 2 * hidden + PAD, :] += lanes(draw)
    dh, dl = split(draw)
    h2h = keep_h[2]
    h2l = keep_h[3]
    both = mm_nt(jnp.concatenate([dh, dl], axis=0), h2h)
    acc3[...] += both[0:PAD] + both[PAD:] + mm_nt(dh, h2l)
    zero = jnp.zeros((256 - 3 * PAD, draw.shape[1]), bf16)
    dh2 = mm(w3b[...], jnp.concatenate([dh, dl, dh, zero], axis=0))
    dz2 = jnp.where(h2h > 0, dh2, 0.0)
    bias[hidden : 2 * hidden, :] += lanes(dz2)
    zh, zl = split(dz2)
    h1h = keep_h[0]
    h1l = keep_h[1]
    both = mm_nt(jnp.concatenate([h1h, h1l], axis=0), zh)
    acc2[...] += both[0:hidden] + both[hidden:] + mm_nt(h1h, zl)
    keep_h[2] = zh
    keep_h[3] = zl


def first_layer_tile(keep_x, keep_h, w2b, acc1, bias):
    hidden = w2b.shape[0]
    feat = keep_x.shape[1]
    h1h = keep_h[0]
    zh = keep_h[2]
    zl = keep_h[3]
    dh1 = mm(w2b[...], jnp.concatenate([zh, zl, zh], axis=0))
    dz1 = jnp.where(h1h > 0, dh1, 0.0)
    bias[0:hidden, :] += lanes(dz1)
    xh = keep_x[0]
    xl = keep_x[1]
    zh, zl = split(dz1)
    both = mm_nt(jnp.concatenate([xh, xl], axis=0), zh)
    acc1[...] += both[0:feat] + both[feat:] + mm_nt(xh, zl)


def step_kernel(
    views, regions,
    feats, spacing, counts, target, rank_ref, w1, b1, w2, b2, w3, b3,
    pixels, total, total_late,
    w1s, w2f, w2b, w3f, w3b, cols, keep_x, keep_h, keep_raw, back, grads, grads_late,
    acc1, acc2, acc3, bias, fsend, frecv, msend, mrecv, nsend, nrecv, gsend, grecv, lsend, lrecv,
    *scratch,
):
    samples, feat, rays = feats.shape
    channels, seg = target.shape
    levels = regions.bit_length() - 1
    rows = back.shape[1]
    hidden = w2.shape[0]
    me = lax.axis_index("depth")
    view = lax.axis_index("view")
    vlevels = views.bit_length() - 1
    work = scratch[0 : levels + 1]
    got = scratch[levels + 1 : 2 * levels + 1]
    notes = scratch[2 * levels + 1 : 3 * levels + 1]
    sums = scratch[3 * levels + 1 :]

    def bit_of(value, b):
        return lax.rem(value // (1 << b), 2)

    def partner(b):
        return {"depth": me + (1 - 2 * bit_of(me, b)) * (1 << b)}

    def view_partner(b):
        return {"view": view + (1 - 2 * bit_of(view, b)) * (1 << b)}

    def peer(r):
        return {"depth": lax.rem(me + r, regions)}

    barrier = pltpu.get_barrier_semaphore()
    for b in range(vlevels):
        pl.semaphore_signal(barrier, inc=1, device_id=view_partner(b), device_id_type=MESH)
    for r in range(1, regions):
        pl.semaphore_signal(barrier, inc=1, device_id=peer(r), device_id_type=MESH)

    prepare(feat, w1, b1, w2, b2, w3, b3, w1s, w2f, w2b, w3f, w3b, cols)
    pl.semaphore_wait(barrier, vlevels + regions - 1)

    def span_of(k):
        where = 0
        for b in range(levels):
            where = where + lax.rem(bit_of(me, b) + bit_of(k, levels - 1 - b), 2) * (1 << b)
        return pl.ds(pl.multiple_of(where * seg, seg), seg)

    rank = rank_ref[0:1, 0:1]

    def first(b):
        return lax.rem(lax.div(rank, jnp.full_like(rank, 1 << b)), jnp.full_like(rank, 2)) == 0

    def color_copy(j, kk):
        n2 = regions >> (j + 1)
        return remote(work[j].at[n2 + kk], got[j].at[kk], (fsend, frecv), n2 + kk, partner(j))

    def misfit_copy(j, kk):
        n2 = regions >> (j + 1)
        part = pl.ds(0, channels)
        return remote(
            back.at[kk, part], back.at[n2 + kk, part], (msend, mrecv), n2 + kk, partner(j)
        )

    def note_copy(j, kk):
        n2 = regions >> (j + 1)
        return remote(
            notes[j].at[kk], back.at[n2 + kk, pl.ds(channels, rows - channels)],
            (nsend, nrecv), n2 + kk, partner(j),
        )

    def gather_x(span):
        return jnp.concatenate([feats[s, :, span] for s in range(samples)], axis=1)

    def forward_step(i, carry):
        k = regions - 1 - i
        span = span_of(k)
        color, depth = forward_tile(
            feat, channels, gather_x(span), [spacing[s, :, span] for s in range(samples)], counts[:, span],
            w1s, w2f, w3f, cols, keep_x.at[k], keep_h.at[k], keep_raw.at[k],
        )
        work[0][k, 0:channels] = color
        work[0][k, channels:rows] = jnp.broadcast_to(depth, (rows - channels, seg))
        for j in range(levels):
            n2 = regions >> (j + 1)

            @pl.when((k >= n2) & (k < 2 * n2))
            def _():
                color_copy(j, k - n2).start()

            @pl.when(k < n2)
            def _():
                color_copy(j, k).wait_recv()
                ahead = first(j)
                mine, other = work[j][k], got[j][k]
                mine_depth = mine[channels : channels + 1]
                other_depth = other[channels : channels + 1]
                mine_clear = jnp.where(ahead, 1.0, jnp.exp(-other_depth))
                other_clear = jnp.where(ahead, jnp.exp(-mine_depth), 1.0)
                work[j + 1][k, 0:channels] = (
                    mine_clear * mine[0:channels] + other_clear * other[0:channels]
                )
                work[j + 1][k, channels:rows] = mine[channels:rows] + other[channels:rows]

        return carry

    lax.fori_loop(0, regions, forward_step, 0)
    color = work[levels][0, 0:channels]
    pixels[...] = color
    row = lax.broadcasted_iota(jnp.int32, (rows - channels, seg), 0)
    back[0, 0:channels] = color - target[...]
    back[0, channels:rows] = jnp.where(row == 0, 1.0, 0.0)
    for acc in (acc1, acc2, acc3, bias):
        acc[...] = jnp.zeros_like(acc)
    order = sorted(range(regions), key=lambda k: (bin(k).count("1"), -k))
    if regions >= 8:
        order = [{3: 5, 5: 3}.get(k, k) for k in order]

    def tile_at(i):
        k = 0
        for at, value in enumerate(order):
            k = k + jnp.where(i == at, value, 0)
        return k

    defer = regions // 2

    def backward_step(i, carry):
        k = tile_at(i)
        for j in range(levels):
            n2 = regions >> (j + 1)

            @pl.when((k >= n2) & (k < 2 * n2))
            def _():
                misfit_copy(j, k - n2).wait_recv()
                note_copy(j, k - n2).wait_recv()

        for j in reversed(range(levels)):
            n2 = regions >> (j + 1)

            @pl.when(k < n2)
            def _():
                misfit_copy(j, k).start()

        for j in reversed(range(levels)):
            n2 = regions >> (j + 1)

            @pl.when(k < n2)
            def _():
                ahead = first(j)
                mine, other = work[j][k], got[j][k]
                misfit = back[k, 0:channels]
                state = back[k, channels:rows]
                passed, behind = state[0:1], state[1:2]
                mine_depth = mine[channels : channels + 1]
                other_depth = other[channels : channels + 1]
                hind = jnp.where(ahead, other[0:channels], mine[0:channels])
                later = passed * jnp.exp(-jnp.where(ahead, mine_depth, other_depth))
                glow = behind + later * jnp.sum(misfit * hind, axis=0, keepdims=True)
                mine_state = (jnp.where(ahead, passed, later), jnp.where(ahead, glow, behind))
                other_state = (jnp.where(ahead, later, passed), jnp.where(ahead, behind, glow))
                notes[j][k] = jnp.where(row == 0, *other_state)
                note_copy(j, k).start()
                back[k, channels:rows] = jnp.where(row == 0, *mine_state)

        span = span_of(k)
        backward_tile(
            channels, keep_raw[k], back[k, 0:channels], back[k, channels:rows],
            [spacing[s, :, span] for s in range(samples)], counts[:, span], keep_h.at[k], w3b,
            acc2, acc3, bias,
        )

        @pl.when(i < defer)
        def _():
            first_layer_tile(keep_x.at[k], keep_h.at[k], w2b, acc1, bias)

        return carry

    lax.fori_loop(0, regions, backward_step, 0)
    for j in range(levels):
        n2 = regions >> (j + 1)
        for kk in range(n2):
            color_copy(j, kk).wait_send()
            misfit_copy(j, kk).wait_send()
            note_copy(j, kk).wait_send()

    count = 2 * vlevels + 1
    early = total_stages(views, regions, grads, total, sums[0:count], (gsend, grecv))
    late = total_stages(views, regions, grads_late, total_late, sums[count:], (lsend, lrecv))
    fill(grads, (acc2, acc3), bias[hidden:, :])
    early[0]()

    def first_layer_step(i, carry):
        k = tile_at(i)
        first_layer_tile(keep_x.at[k], keep_h.at[k], w2b, acc1, bias)

        @pl.when(i == defer)
        def _():
            early[1]()

        return carry

    lax.fori_loop(defer, regions, first_layer_step, 0)
    fill(grads_late, (acc1,), bias[0:hidden, :])
    early = early[2:]
    for which in "LELLELELELL" + "EL" * (2 * len(late)):
        queue = early if which == "E" else late
        if queue:
            queue.pop(0)()


def whole_step(views, regions, feats, spacing, counts, target, rank, weights):
    samples, feat, rays = feats.shape
    channels, seg = target.shape
    hidden = weights[2].shape[0]
    levels = regions.bit_length() - 1
    vlevels = views.bit_length() - 1
    rows = channels + 8
    wide = samples * seg
    devices = views * regions
    sizes = block_counts(feat, hidden, devices)
    scratch = [
        pltpu.VMEM((hidden, 128), bf16),
        pltpu.VMEM((hidden, 3 * hidden), bf16),
        pltpu.VMEM((hidden, 3 * hidden), bf16),
        pltpu.VMEM((2 * PAD, hidden), bf16),
        pltpu.VMEM((hidden, 256), bf16),
        pltpu.VMEM((hidden, hidden), f32),
        pltpu.VMEM((regions, 2, feat, wide), bf16),
        pltpu.VMEM((regions, 4, hidden, wide), bf16),
        pltpu.VMEM((regions, PAD, wide), f32),
        pltpu.VMEM((regions, rows, seg), f32),
        pltpu.VMEM((sizes[0], 8, 128), f32),
        pltpu.VMEM((sizes[1], 8, 128), f32),
        pltpu.VMEM((feat, hidden), f32),
        pltpu.VMEM((hidden, hidden), f32),
        pltpu.VMEM((PAD, hidden), f32),
        pltpu.VMEM((3 * hidden, 128), f32),
    ]
    scratch += [pltpu.SemaphoreType.DMA((regions,))] * 6
    scratch += [pltpu.SemaphoreType.DMA((2 * (vlevels + regions - 1),))] * 4
    scratch += [pltpu.VMEM((regions >> j, rows, seg), f32) for j in range(levels + 1)]
    scratch += [pltpu.VMEM((regions >> (j + 1), rows, seg), f32) for j in range(levels)]
    scratch += [pltpu.VMEM((regions >> (j + 1), 8, seg), f32) for j in range(levels)]
    for blocks in sizes:
        for b in range(vlevels):
            scratch += [pltpu.VMEM((blocks >> (b + 1), 8, 128), f32)] * 2
        scratch.append(pltpu.VMEM((regions - 1, blocks // devices, 8, 128), f32))
    vmem = pl.BlockSpec(memory_space=pltpu.VMEM)
    return pl.pallas_call(
        functools.partial(step_kernel, views, regions),
        in_specs=[vmem] * 11,
        out_specs=[vmem] * 3,
        out_shape=[
            jax.ShapeDtypeStruct((channels, seg), f32),
            jax.ShapeDtypeStruct((sizes[0], 8, 128), f32),
            jax.ShapeDtypeStruct((sizes[1], 8, 128), f32),
        ],
        scratch_shapes=scratch,
        compiler_params=pltpu.CompilerParams(
            collective_id=0, has_side_effects=True, vmem_limit_bytes=66000000
        ),
        name="whole_step",
    )(feats, spacing, counts, target, rank, *weights)


def finish_kernel(
    feat, hidden, outs,
    pixels_in, total, late,
    pixels, first_update, first_shift, second_update, second_shift, last_update, last_shift,
):
    def scaled(value, count):
        square = jnp.sum(jnp.sum(value * value, axis=0, keepdims=True), axis=1, keepdims=True)
        return value / jnp.sqrt(square / count + epsilon)

    pixels[...] = pixels_in[...]

    def join(source, at, rows):
        halves = []
        for _ in range(0, hidden, 128):
            halves.append(source[at : at + rows // 8].reshape(rows, 128))
            at += rows // 8
        return jnp.concatenate(halves, axis=1), at

    second, at = join(total, 0, hidden)
    last, at = join(total, at, PAD)
    first, late_at = join(late, 0, feat)
    second_update[...] = scaled(second, hidden * hidden)
    first_update[...] = scaled(first, feat * hidden)
    last_update[...] = scaled(last, hidden * outs)[0:outs]
    across = hidden // 128
    rows = total[at]
    late_rows = late[late_at]
    wide = lambda rows: jnp.concatenate([rows[i : i + 1] for i in range(across)], axis=1)
    first_shift[...] = scaled(wide(late_rows), hidden)
    second_shift[...] = scaled(wide(rows), hidden)
    last_shift[...] = scaled(rows[across : across + 1], outs)[:, 0:outs]


def finish(pixels, total, late, feat, hidden, outs):
    vmem = pl.BlockSpec(memory_space=pltpu.VMEM)
    shapes = [
        pixels.shape, (feat, hidden), (1, hidden), (hidden, hidden), (1, hidden),
        (outs, hidden), (1, outs),
    ]
    return pl.pallas_call(
        functools.partial(finish_kernel, feat, hidden, outs),
        in_specs=[vmem] * 3,
        out_specs=[vmem] * len(shapes),
        out_shape=[jax.ShapeDtypeStruct(shape, f32) for shape in shapes],
        name="normalize_all",
    )(pixels, total, late)


def local(
    features, spacing, counts, depth_rank, target,
    first_weight, first_bias, second_weight, second_bias, last_weight, last_bias,
):
    regions = lax.axis_size("depth")
    views = lax.axis_size("view")
    feat, hidden = first_weight.shape
    outs = last_weight.shape[1]
    feats, gaps, live = jnp.transpose(features[0, 0], (1, 0, 2)), jnp.transpose(spacing[0], (1, 0, 2)), counts[0]
    weights = (
        first_weight, first_bias[None], second_weight, second_bias[None],
        last_weight.T, last_bias[None],
    )
    pixels, total, late = whole_step(views, regions, feats, gaps, live, target[0], depth_rank, weights)
    results = finish(pixels, total, late, feat, hidden, outs)
    return (
        results[0][None], results[1], results[2][0], results[3], results[4][0],
        results[5].T, results[6][0],
    )


def solution(mesh):
    return jax.shard_map(
        local,
        mesh=mesh,
        in_specs=(
            P("view", "depth", None, None, None),
            P("view", "depth", None, None),
            P("view", "depth", None),
            P("view", "depth"),
            P("view", None, "depth"),
            P(), P(), P(), P(), P(), P(),
        ),
        out_specs=(P("view", None, "depth"), P(), P(), P(), P(), P(), P()),
        check_vma=False,
    )
```
